32 devices in a mesh: row: 8 (over y, x, core), col: 4 (over z).
Axes of the slice: x: 2, y: 2, z: 4, core: 2. Of those that a mesh axis runs over, the one named last changes fastest.
Arguments:
- matrix: float32 [10240, 10240], P('row', 'col'), may hold values from 0 to 1.5, as said below
Outputs:
- factored: float32 [10240, 10240], P('row', 'col')
The draws below stay inside these ranges and needn't reach their ends.
Inputs may be any that keep to these rules, and one draw needn't show every extreme that they name: A Gaussian kernel matrix over random embeddings plus a ridge on the diagonal, stored block-cyclically; symmetric positive definite, diagonal entries near 1.5.
All inputs are finite; a program needn't handle non-finite values.
Results may differ from the reference program's by a relative error of at most 0.0003.
Values sent between devices are 32-bit elements; how exact they have to be, the bound alone decides.
A program may use at most 192 MiB of HBM per device.

```python
import jax
import jax.numpy as jnp
from jax import lax

NB = 256
TR = 5
TC = 10
N_ROW = 8
N_COL = 4


ridge_term = 0.5


def draw_matrix(key, part):
    key_emb, key_scale = jax.random.split(jax.random.fold_in(key, 11))
    emb_dim = 64
    total = TR * NB * N_ROW
    points = jax.random.normal(key_emb, (total, emb_dim), jnp.float32)
    scales = jnp.exp(jax.random.uniform(key_scale, (total,), jnp.float32, jnp.log(0.5), jnp.log(1.5)))
    points = points * scales[:, None]
    sq_norm = jnp.sum(points * points, axis=1)
    dist_sq = sq_norm[:, None] + sq_norm[None, :] - 2.0 * jnp.dot(points, points.T, precision=lax.Precision.HIGHEST)
    dist_sq = jnp.maximum(dist_sq, 0.0)
    kernel = jnp.exp(-dist_sq / (2.0 * 0.8 * emb_dim))
    kernel = 0.5 * (kernel + kernel.T)
    full = kernel + ridge_term * jnp.eye(total, dtype=jnp.float32)
    rows = full.reshape(TR, N_ROW, NB, total).transpose(1, 0, 2, 3).reshape(total, total)
    return rows.reshape(total, TC, N_COL, NB).transpose(0, 2, 1, 3).reshape(total, total)


def setup_inputs(seed: int = 0) -> dict:
    seeds = jax.random.split(jax.random.key(seed), 2)
    matrix = draw_matrix(jax.random.fold_in(seeds[1], 71), 0)
    return {"matrix": matrix}


def to_global(stored):
    total = stored.shape[0]
    rows = stored.reshape(N_ROW, TR, NB, total).transpose(1, 0, 2, 3).reshape(total, total)
    return rows.reshape(total, N_COL, TC, NB).transpose(0, 2, 1, 3).reshape(total, total)

def to_storage(matrix):
    total = matrix.shape[0]
    rows = matrix.reshape(TR, N_ROW, NB, total).transpose(1, 0, 2, 3).reshape(total, total)
    return rows.reshape(total, TC, N_COL, NB).transpose(0, 2, 1, 3).reshape(total, total)

def factor(block):
    low_part = jnp.linalg.cholesky(block[:NB, :NB])
    inverse = lax.linalg.triangular_solve(low_part, jnp.eye(NB, dtype=low_part.dtype), left_side=True, lower=True)
    panel = jnp.dot(block[NB:, :NB], inverse.T, precision=lax.Precision.HIGHEST)
    return (low_part, panel)

def reference(matrix):
    global_form = to_global(matrix)
    total = global_form.shape[0]
    low_first, pan_first = factor(global_form)
    schur_one = global_form[NB:, NB:] - jnp.dot(pan_first, pan_first.T, precision=lax.Precision.HIGHEST)
    low_second, pan_second = factor(schur_one)
    schur_two = schur_one[NB:, NB:] - jnp.dot(pan_second, pan_second.T, precision=lax.Precision.HIGHEST)
    result = jnp.zeros((total, total), global_form.dtype)
    result = result.at[:NB, :NB].set(low_first)
    result = result.at[NB:, :NB].set(pan_first)
    result = result.at[NB:2 * NB, NB:2 * NB].set(low_second)
    result = result.at[2 * NB:, NB:2 * NB].set(pan_second)
    result = result.at[2 * NB:, 2 * NB:].set(schur_two)
    return to_storage(result)
```

```python
import functools
import jax
import jax.numpy as jnp
from jax import lax
from jax.experimental import pallas as pl
from jax.experimental.pallas import tpu as pltpu
from jax.sharding import PartitionSpec as P

NB = 256
BK = 32
MESH = pl.DeviceIdType.MESH
HIGH = lax.Precision.HIGHEST


def dot(a, b, dims=((1,), (0,))):
    return lax.dot_general(a, b, (dims, ((), ())), precision=HIGH, preferred_element_type=jnp.float32)


def factor_block(work, lt_ref, v_ref, k):
    base = pl.multiple_of(k * BK, BK)
    rows = work[pl.ds(base, BK), :]
    lead = pltpu.roll(rows[:, :NB], lax.rem(NB - base, NB), 1)[:, :128]
    lane = lax.broadcasted_iota(jnp.int32, (BK, 128), 1)
    sub = lax.broadcasted_iota(jnp.int32, (BK, 128), 0)
    w = jnp.where(lane < BK, lead, jnp.where(lane == sub + BK, 1.0, 0.0))
    scale = jnp.ones((BK, 128), jnp.float32)
    for j in range(0, BK, 2):
        c0 = jnp.broadcast_to(w[:, j:j + 1], (BK, 128))
        c1 = jnp.broadcast_to(w[:, j + 1:j + 2], (BK, 128))
        r0 = jnp.broadcast_to(w[j:j + 1, :], (BK, 128))
        r1 = jnp.broadcast_to(w[j + 1:j + 2, :], (BK, 128))
        d = jnp.broadcast_to(c0[j:j + 1, :], (BK, 128))
        e = jnp.broadcast_to(c0[j + 1:j + 2, :], (BK, 128))
        f = jnp.broadcast_to(c1[j + 1:j + 2, :], (BK, 128))
        inv_d = 1.0 / d
        inv_f = d / (f * d - e * e)
        ratio = e * inv_d
        m0 = jnp.where(sub > j, c0 * inv_d, 0.0)
        r1n = r1 - ratio * r0
        m1 = jnp.where(sub > j + 1, (c1 - ratio * c0) * inv_f, 0.0)
        w = w - m0 * r0 - m1 * r1n
        scale = jnp.where(sub == j, inv_d, jnp.where(sub == j + 1, inv_f, scale))
    w = w * jnp.sqrt(scale)
    vd = pltpu.roll(w, 128 - BK, 1)[:, :BK]
    new = dot(vd, rows)
    wide = lax.broadcasted_iota(jnp.int32, (BK, NB), 1)
    tall = lax.broadcasted_iota(jnp.int32, (BK, NB), 0)
    top = jnp.where(wide >= tall + base, new[:, :NB], 0.0)
    lt_ref[pl.ds(base, BK), :] = top
    v_ref[pl.ds(base, BK), :] = new[:, NB:]
    left = jnp.where(wide >= base + BK, top, 0.0)
    right = jnp.concatenate([top, new[:, NB:]], axis=1)
    work[...] = work[...] - dot(left, right, ((0,), (0,)))


def set_work(work, tile):
    work[:, :NB] = tile
    a = lax.broadcasted_iota(jnp.int32, (NB, NB), 0)
    b = lax.broadcasted_iota(jnp.int32, (NB, NB), 1)
    work[:, NB:] = jnp.where(a == b, 1.0, 0.0)


def pick(index, table):
    out = jnp.int32(0)
    for i, value in enumerate(table):
        out = out + jnp.where(index == i, jnp.int32(value), jnp.int32(0))
    return out


def chain_kernel(n_row, n_col, chunks, a_ref, r_out, c_out, v_out, lt_out, mid_out,
                 rbuf, cbuf, dbuf, work, r_send, r_recv, c_send, c_recv, d_send, d_recv, loc):
    row = lax.axis_index("row")
    col = lax.axis_index("col")
    n_rows = rbuf.shape[1]
    n_cols = cbuf.shape[2]
    r_step = n_rows // chunks
    c_step = n_cols // chunks
    half = n_row // 2
    order = [i ^ (i >> 1) for i in range(half)]
    orders = [order, order[:1] + order[:0:-1]]
    pair = row // 2
    core = lax.rem(row, 2)
    sibling = row + 1 - 2 * core
    nexts, hops, lasts = [], [], []
    for k in range(2):
        table = [0] * half
        where = [0] * half
        for i, q in enumerate(orders[k]):
            table[q] = orders[k][(i + 1) % half]
            where[q] = i
        nexts.append(2 * pick(pair, table) + k)
        place = pick(pair, where)
        hops.append(jnp.where(core == k, place, place + 1))
        lasts.append(place == half - 1)

    def remote(src, ssem, rsem, target):
        return pltpu.make_async_remote_copy(
            src_ref=src, dst_ref=src, send_sem=ssem, recv_sem=rsem, device_id=target, device_id_type=MESH)

    def local(src, dst, sem):
        return pltpu.make_async_copy(src, dst, sem)

    own = []
    for k in range(2):
        own.append((col == k, local(a_ref.at[:, pl.ds(0, NB)], rbuf.at[k], loc.at[2 * k])))
        own.append((row == k, local(a_ref.at[pl.ds(0, NB), :], cbuf.at[k], loc.at[2 * k + 1])))
    roots = ((0, 0), (1, 0), (1, 1))
    for i, (a, b) in enumerate(roots):
        own.append(((row == a) & (col == b), local(a_ref.at[pl.ds(0, NB), pl.ds(0, NB)], dbuf.at[i], loc.at[4 + i])))
    for cond, copy in own:
        pl.when(cond)(copy.start)

    barrier = pltpu.get_barrier_semaphore()
    for i in range(1, n_row):
        pl.semaphore_signal(barrier, inc=1, device_id=(lax.rem(row + i, n_row), col), device_id_type=MESH)
    for i in range(1, n_col):
        pl.semaphore_signal(barrier, inc=1, device_id=(row, lax.rem(col + i, n_col)), device_id_type=MESH)
    pl.semaphore_wait(barrier, n_row + n_col - 2)
    for cond, copy in own:
        pl.when(cond)(copy.wait)

    d_sends = []
    for i, (a, b) in enumerate(roots):
        tile = dbuf.at[i]
        k = a
        root = (row == a) & (col == b)
        recv = remote(tile, d_send.at[i, 0], d_recv.at[i], (row, col))
        pl.when(jnp.logical_not(root))(recv.wait_recv)
        up = (row == a) & (col >= b) & (col < n_col - 1)
        down = (row == a) & (col <= b) & (col > 0)
        sends = (
            (up, remote(tile, d_send.at[i, 0], d_recv.at[i], (row, jnp.minimum(col + 1, n_col - 1)))),
            (down, remote(tile, d_send.at[i, 1], d_recv.at[i], (row, jnp.maximum(col - 1, 0)))),
            ((core == k) & jnp.logical_not(lasts[k]), remote(tile, d_send.at[i, 2], d_recv.at[i], (nexts[k], col))),
            (core == k, remote(tile, d_send.at[i, 3], d_recv.at[i], (sibling, col))),
        )
        for cond, copy in sends:
            pl.when(cond)(copy.start)
        d_sends.extend(sends)

    def r_piece(k, c):
        return rbuf.at[k, pl.ds(pl.multiple_of(c * r_step, r_step), r_step), :]

    def c_piece(k, c):
        return cbuf.at[k, :, pl.ds(pl.multiple_of(c * c_step, c_step), c_step)]

    def r_sends(k, c):
        piece = r_piece(k, c)
        return (
            ((col >= k) & (col < n_col - 1),
             remote(piece, r_send.at[k, 0, c], r_recv.at[k, c], (row, jnp.minimum(col + 1, n_col - 1)))),
            ((col <= k) & (col > 0),
             remote(piece, r_send.at[k, 1, c], r_recv.at[k, c], (row, jnp.maximum(col - 1, 0)))),
        )

    def c_sends(k, c):
        piece = c_piece(k, c)
        return (
            ((core == k) & jnp.logical_not(lasts[k]),
             remote(piece, c_send.at[k, 0, c], c_recv.at[k, c], (nexts[k], col))),
            (core == k, remote(piece, c_send.at[k, 1, c], c_recv.at[k, c], (sibling, col))),
        )

    def pump(s):
        for k in range(2):
            far = jnp.where(col >= k, col - k, k - col)

            def r_one(c, k=k, far=far):
                pl.when(far > 0)(remote(r_piece(k, c), r_send.at[k, 0, c], r_recv.at[k, c], (row, col)).wait_recv)
                for cond, copy in r_sends(k, c):
                    pl.when(cond)(copy.start)

            def c_one(c, k=k):
                pl.when(row != k)(remote(c_piece(k, c), c_send.at[k, 0, c], c_recv.at[k, c], (row, col)).wait_recv)
                for cond, copy in c_sends(k, c):
                    pl.when(cond)(copy.start)

            pl.when((s >= far) & (s < far + chunks))(lambda: r_one(s - far))
            hop = hops[k]
            pl.when((s >= hop) & (s < hop + chunks))(lambda: c_one(s - hop))

    blocks = NB // BK
    set_work(work, dbuf[0])

    def first(s, carry):
        pump(s)
        factor_block(work, lt_out.at[0], v_out.at[0], s)
        return carry

    lax.fori_loop(0, blocks, first, 0)
    mid = dot(dbuf[1], v_out[0], ((1,), (1,)))
    mid_out[...] = mid
    set_work(work, dbuf[2] - dot(mid, mid, ((1,), (1,))))

    def second(s, carry):
        pump(s + blocks)
        factor_block(work, lt_out.at[1], v_out.at[1], s)
        return carry

    lax.fori_loop(0, blocks, second, 0)

    total = chunks + max(n_col, half + 1)
    if total > 2 * blocks:
        def rest(s, carry):
            pump(s)
            return carry

        lax.fori_loop(2 * blocks, total, rest, 0)

    back = [local(rbuf, r_out, loc.at[0]), local(cbuf, c_out, loc.at[1])]
    for copy in back:
        copy.start()
    for cond, copy in d_sends:
        pl.when(cond)(copy.wait_send)

    def drain(c, carry):
        for k in range(2):
            for cond, copy in r_sends(k, c) + c_sends(k, c):
                pl.when(cond)(copy.wait_send)
        return carry

    lax.fori_loop(0, chunks, drain, 0)
    for copy in back:
        copy.wait()


def halves(x):
    hi = x.astype(jnp.bfloat16)
    lo = (x - hi.astype(jnp.float32)).astype(jnp.bfloat16)
    return hi, lo


def update_kernel(n_row, n_col, a_ref, r_ref, c_ref, v_ref, lt_ref, mid_ref, o_ref, right):
    t = pl.program_id(0)
    row = lax.axis_index("row")
    col = lax.axis_index("col")
    n_cols = a_ref.shape[1]

    @pl.when(t == 0)
    def _():
        @pl.loop(0, n_cols // NB)
        def _(s):
            span = pl.ds(pl.multiple_of(s * NB, NB), NB)
            p0 = dot(v_ref[0], c_ref[0, :, span])
            p1 = dot(v_ref[1], c_ref[1, :, span] - dot(mid_ref[...], p0))
            for k, p in enumerate((p0, p1)):
                hi, lo = halves(p)
                right[pl.ds(3 * k * NB, NB), span] = hi
                right[pl.ds((3 * k + 1) * NB, NB), span] = lo
                right[pl.ds((3 * k + 2) * NB, NB), span] = hi

    g = t * n_row + row
    q0 = dot(r_ref[0], v_ref[0], ((1,), (1,)))
    q1 = dot(r_ref[1] - dot(q0, mid_ref[...], ((1,), (1,))), v_ref[1], ((1,), (1,)))
    h0, l0 = halves(q0)
    h1, l1 = halves(q1)
    left = jnp.concatenate([h0, h0, l0, h1, h1, l1], axis=1)
    wide = 2 * NB if n_cols % (2 * NB) == 0 else NB

    @pl.loop(0, n_cols // wide)
    def _(s):
        span = pl.ds(pl.multiple_of(s * wide, wide), wide)
        o_ref[:, span] = a_ref[:, span] - lax.dot_general(
            left, right[:, span], (((1,), (0,)), ((), ())), preferred_element_type=jnp.float32)

    @pl.when(g < 2)
    def _():
        o_ref[...] = jnp.zeros_like(o_ref)

    @pl.when(col == 0)
    def _():
        o_ref[:, :NB] = q0

        @pl.when(g == 0)
        def _():
            o_ref[:, :NB] = lt_ref[0].T

    @pl.when((col == 1) & (g > 0))
    def _():
        o_ref[:, :NB] = q1

        @pl.when(g == 1)
        def _():
            o_ref[:, :NB] = lt_ref[1].T


def body(n_row, n_col, matrix):
    n_rows, n_cols = matrix.shape
    chunks = 10
    f32 = jnp.float32
    anyspace = pl.BlockSpec(memory_space=pl.ANY)
    vmem = pl.BlockSpec(memory_space=pltpu.VMEM)
    r, c, v, lt, mid = pl.pallas_call(
        functools.partial(chain_kernel, n_row, n_col, chunks),
        out_shape=(
            jax.ShapeDtypeStruct((2, n_rows, NB), f32),
            jax.ShapeDtypeStruct((2, NB, n_cols), f32),
            jax.ShapeDtypeStruct((2, NB, NB), f32),
            jax.ShapeDtypeStruct((2, NB, NB), f32),
            jax.ShapeDtypeStruct((NB, NB), f32),
        ),
        in_specs=[anyspace],
        out_specs=(anyspace, anyspace, vmem, vmem, vmem),
        scratch_shapes=[
            pltpu.VMEM((2, n_rows, NB), f32),
            pltpu.VMEM((2, NB, n_cols), f32),
            pltpu.VMEM((3, NB, NB), f32),
            pltpu.VMEM((NB, 2 * NB), f32),
            pltpu.SemaphoreType.DMA((2, 2, chunks)),
            pltpu.SemaphoreType.DMA((2, chunks)),
            pltpu.SemaphoreType.DMA((2, 2, chunks)),
            pltpu.SemaphoreType.DMA((2, chunks)),
            pltpu.SemaphoreType.DMA((3, 4)),
            pltpu.SemaphoreType.DMA((3,)),
            pltpu.SemaphoreType.DMA((7,)),
        ],
        compiler_params=pltpu.CompilerParams(
            collective_id=0, has_side_effects=True, vmem_limit_bytes=24 * 2**20),
        name="chain",
    )(matrix)
    whole = lambda shape: pl.BlockSpec(shape, lambda t: (0,) * len(shape), pipeline_mode=pl.Buffered(1))
    return pl.pallas_call(
        functools.partial(update_kernel, n_row, n_col),
        grid=(n_rows // NB,),
        out_shape=jax.ShapeDtypeStruct(matrix.shape, f32),
        in_specs=[
            pl.BlockSpec((NB, n_cols), lambda t: (t, 0)),
            pl.BlockSpec((2, NB, NB), lambda t: (0, t, 0)),
            whole((2, NB, n_cols)),
            whole((2, NB, NB)),
            whole((2, NB, NB)),
            whole((NB, NB)),
        ],
        out_specs=pl.BlockSpec((NB, n_cols), lambda t: (t, 0)),
        scratch_shapes=[pltpu.VMEM((6 * NB, n_cols), jnp.bfloat16)],
        compiler_params=pltpu.CompilerParams(vmem_limit_bytes=48 * 2**20),
        name="update",
    )(matrix, r, c, v, lt, mid)


def solution(mesh):
    n_row, n_col = mesh.shape["row"], mesh.shape["col"]
    return jax.shard_map(
        functools.partial(body, n_row, n_col), mesh=mesh,
        in_specs=(P("row", "col"),), out_specs=P("row", "col"), check_vma=False)
```

```python
import functools
import jax
import jax.numpy as jnp
from jax import lax
from jax.experimental import pallas as pl
from jax.experimental.pallas import tpu as pltpu
from jax.sharding import PartitionSpec as P

NB = 256
BK = 32
PIECES = 4
MESH = pl.DeviceIdType.MESH
HIGH = lax.Precision.HIGHEST


def dot(a, b, dims=((1,), (0,))):
    return lax.dot_general(a, b, (dims, ((), ())), precision=HIGH, preferred_element_type=jnp.float32)


def factor_block(work, lt_ref, v_ref, k):
    base = pl.multiple_of(k * BK, BK)
    rows = work[pl.ds(base, BK), :]
    lead = pltpu.roll(rows[:, :NB], lax.rem(NB - base, NB), 1)[:, :128]
    lane = lax.broadcasted_iota(jnp.int32, (BK, 128), 1)
    sub = lax.broadcasted_iota(jnp.int32, (BK, 128), 0)
    w = jnp.where(lane < BK, lead, jnp.where(lane == sub + BK, 1.0, 0.0))
    scale = jnp.ones((BK, 128), jnp.float32)
    for j in range(0, BK, 2):
        c0 = jnp.broadcast_to(w[:, j:j + 1], (BK, 128))
        c1 = jnp.broadcast_to(w[:, j + 1:j + 2], (BK, 128))
        r0 = jnp.broadcast_to(w[j:j + 1, :], (BK, 128))
        r1 = jnp.broadcast_to(w[j + 1:j + 2, :], (BK, 128))
        d = jnp.broadcast_to(c0[j:j + 1, :], (BK, 128))
        e = jnp.broadcast_to(c0[j + 1:j + 2, :], (BK, 128))
        f = jnp.broadcast_to(c1[j + 1:j + 2, :], (BK, 128))
        inv_d = 1.0 / d
        inv_f = d / (f * d - e * e)
        ratio = e * inv_d
        m0 = jnp.where(sub > j, c0 * inv_d, 0.0)
        r1n = r1 - ratio * r0
        m1 = jnp.where(sub > j + 1, (c1 - ratio * c0) * inv_f, 0.0)
        w = w - m0 * r0 - m1 * r1n
        scale = jnp.where(sub == j, inv_d, jnp.where(sub == j + 1, inv_f, scale))
    w = w * jnp.sqrt(scale)
    vd = pltpu.roll(w, 128 - BK, 1)[:, :BK]
    new = dot(vd, rows)
    wide = lax.broadcasted_iota(jnp.int32, (BK, NB), 1)
    tall = lax.broadcasted_iota(jnp.int32, (BK, NB), 0)
    top = jnp.where(wide >= tall + base, new[:, :NB], 0.0)
    lt_ref[pl.ds(base, BK), :] = top
    v_ref[pl.ds(base, BK), :] = new[:, NB:]
    left = jnp.where(wide >= base + BK, top, 0.0)
    right = jnp.concatenate([top, new[:, NB:]], axis=1)
    work[...] = work[...] - dot(left, right, ((0,), (0,)))


def set_work(work, tile):
    work[:, :NB] = tile
    a = lax.broadcasted_iota(jnp.int32, (NB, NB), 0)
    b = lax.broadcasted_iota(jnp.int32, (NB, NB), 1)
    work[:, NB:] = jnp.where(a == b, 1.0, 0.0)


def pick(index, table):
    out = jnp.int32(0)
    for i, value in enumerate(table):
        out = out + jnp.where(index == i, jnp.int32(value), jnp.int32(0))
    return out


def chain_kernel(n_row, n_col, chunks, a_ref, r_out, c_out, v_out, lt_out, mid_out,
                 rbuf, cbuf, dbuf, work, r_send, r_recv, c_send, c_recv, d_send, d_recv, loc):
    row = lax.axis_index("row")
    col = lax.axis_index("col")
    n_rows = rbuf.shape[1]
    n_cols = cbuf.shape[2]
    r_step = n_rows // chunks
    c_step = n_cols // chunks
    half = n_row // 2
    order = [i ^ (i >> 1) for i in range(half)]
    orders = [order, order[:1] + order[:0:-1]]
    pair = row // 2
    core = lax.rem(row, 2)
    sibling = row + 1 - 2 * core
    nexts, hops, lasts, prevs, fwd, bwd, ring_hops = [], [], [], [], [], [], []
    for k in range(2):
        table, where, before = [0] * half, [0] * half, [0] * half
        for i, q in enumerate(orders[k]):
            table[q] = orders[k][(i + 1) % half]
            before[q] = orders[k][(i - 1) % half]
            where[q] = i
        place = pick(pair, where)
        nexts.append(2 * pick(pair, table) + k)
        prevs.append(2 * pick(pair, before) + k)
        hops.append(jnp.where(core == k, place, place + 1))
        lasts.append(place == half - 1)
        fwd.append((core == k) & (place < half // 2))
        bwd.append((core == k) & ((place == 0) | (place > half // 2 + 1)))
        near = jnp.where(place <= half // 2, place, half - place)
        ring_hops.append(jnp.where(core == k, near, near + 1))

    def remote(src, ssem, rsem, target):
        return pltpu.make_async_remote_copy(
            src_ref=src, dst_ref=src, send_sem=ssem, recv_sem=rsem, device_id=target, device_id_type=MESH)

    def local(src, dst, sem):
        return pltpu.make_async_copy(src, dst, sem)

    own = []
    for k in range(2):
        own.append((col == k, local(a_ref.at[:, pl.ds(0, NB)], rbuf.at[k], loc.at[2 * k])))
        own.append((row == k, local(a_ref.at[pl.ds(0, NB), :], cbuf.at[k], loc.at[2 * k + 1])))
    roots = ((0, 0), (1, 0), (1, 1))
    for i, (a, b) in enumerate(roots):
        own.append(((row == a) & (col == b), local(a_ref.at[pl.ds(0, NB), pl.ds(0, NB)], dbuf.at[i], loc.at[4 + i])))
    for cond, copy in own:
        pl.when(cond)(copy.start)

    barrier = pltpu.get_barrier_semaphore()
    for i in range(1, n_row):
        pl.semaphore_signal(barrier, inc=1, device_id=(lax.rem(row + i, n_row), col), device_id_type=MESH)
    for i in range(1, n_col):
        pl.semaphore_signal(barrier, inc=1, device_id=(row, lax.rem(col + i, n_col)), device_id_type=MESH)
    pl.semaphore_wait(barrier, n_row + n_col - 2)
    for cond, copy in own:
        pl.when(cond)(copy.wait)

    d_step = NB // PIECES

    def d_sends(i, p):
        a, b = roots[i]
        k = a
        tile = dbuf.at[i, pl.ds(pl.multiple_of(p * d_step, d_step), d_step), :]
        up = (row == a) & (col >= b) & (col < n_col - 1)
        down = (row == a) & (col <= b) & (col > 0)
        return tile, (
            (up, remote(tile, d_send.at[i, 0, p], d_recv.at[i, p], (row, jnp.minimum(col + 1, n_col - 1)))),
            (down, remote(tile, d_send.at[i, 1, p], d_recv.at[i, p], (row, jnp.maximum(col - 1, 0)))),
            (fwd[k], remote(tile, d_send.at[i, 2, p], d_recv.at[i, p], (nexts[k], col))),
            (bwd[k], remote(tile, d_send.at[i, 3, p], d_recv.at[i, p], (prevs[k], col))),
            (core == k, remote(tile, d_send.at[i, 4, p], d_recv.at[i, p], (sibling, col))),
        )

    def d_relay(i):
        a, b = roots[i]

        def step(p, carry):
            tile, sends = d_sends(i, p)
            pl.when((row != a) | (col != b))(
                remote(tile, d_send.at[i, 0, p], d_recv.at[i, p], (row, col)).wait_recv)
            for cond, copy in sends:
                pl.when(cond)(copy.start)
            return carry

        lax.fori_loop(0, PIECES, step, 0)

    def r_piece(k, c):
        return rbuf.at[k, pl.ds(pl.multiple_of(c * r_step, r_step), r_step), :]

    def c_piece(k, c):
        return cbuf.at[k, :, pl.ds(pl.multiple_of(c * c_step, c_step), c_step)]

    def r_sends(k, c):
        piece = r_piece(k, c)
        return (
            ((col >= k) & (col < n_col - 1),
             remote(piece, r_send.at[k, 0, c], r_recv.at[k, c], (row, jnp.minimum(col + 1, n_col - 1)))),
            ((col <= k) & (col > 0),
             remote(piece, r_send.at[k, 1, c], r_recv.at[k, c], (row, jnp.maximum(col - 1, 0)))),
        )

    def c_sends(k, c):
        piece = c_piece(k, c)
        return (
            ((core == k) & jnp.logical_not(lasts[k]),
             remote(piece, c_send.at[k, 0, c], c_recv.at[k, c], (nexts[k], col))),
            (core == k, remote(piece, c_send.at[k, 1, c], c_recv.at[k, c], (sibling, col))),
        )

    early = chunks // 2

    def r_root(k):
        def step(c, carry):
            up, down = r_sends(k, c)
            pl.when((col == k) & up[0] & ((k == 0) | (c < early)))(up[1].start)
            pl.when((col == k) & down[0])(down[1].start)
            return carry

        lax.fori_loop(0, chunks, step, 0)

    def c_root(k):
        def step(c, carry):
            for cond, copy in c_sends(k, c):
                pl.when((row == k) & cond)(copy.start)
            return carry

        lax.fori_loop(0, chunks, step, 0)

    def pump(s, tiles=True):
        if tiles:
            for i in (1, 2):
                pl.when((row != roots[i][0]) & (s == ring_hops[roots[i][0]]))(lambda i=i: d_relay(i))
        for k in range(2):
            far = jnp.where(col >= k, col - k, k - col)

            def r_one(c, k=k):
                pl.when(col != k)(remote(r_piece(k, c), r_send.at[k, 0, c], r_recv.at[k, c], (row, col)).wait_recv)
                for cond, copy in r_sends(k, c):
                    pl.when((col != k) & cond)(copy.start)
                if k == 1:
                    @pl.when((col == k) & (c < chunks - early))
                    def _():
                        cond, copy = r_sends(k, c + early)[0]
                        pl.when(cond)(copy.start)

            def c_one(c, k=k):
                remote(c_piece(k, c), c_send.at[k, 0, c], c_recv.at[k, c], (row, col)).wait_recv()
                for cond, copy in c_sends(k, c):
                    pl.when(cond)(copy.start)

            u = s - far
            c = (5 * jnp.maximum(u, 0) + 6) // 7
            pl.when((u >= 0) & ((7 * c) // 5 == u) & (c < chunks))(lambda: r_one(c))
            hop = hops[k]
            pl.when((s >= hop) & (s < hop + chunks) & (row != k))(lambda: c_one(s - hop))

    pl.when(row > 1)(lambda: [r_root(k) for k in range(2)] and None)
    d_relay(0)
    pl.when(row == 1)(lambda: [d_relay(i) for i in (1, 2)] and None)
    pl.when(row <= 1)(lambda: [r_root(k) for k in range(2)] and None)
    for k in range(2):
        pl.when(row == k)(functools.partial(c_root, k))

    blocks = NB // BK
    set_work(work, dbuf[0])

    def first(s, carry):
        pump(s)
        factor_block(work, lt_out.at[0], v_out.at[0], s)
        return carry

    lax.fori_loop(0, blocks, first, 0)
    most = half // 2 + 2
    if most > blocks:
        def tiles_rest(s, carry):
            for i in (1, 2):
                pl.when((row != roots[i][0]) & (s == ring_hops[roots[i][0]]))(lambda i=i: d_relay(i))
            return carry

        lax.fori_loop(blocks, most, tiles_rest, 0)
    mid = dot(dbuf[1], v_out[0], ((1,), (1,)))
    mid_out[...] = mid
    set_work(work, dbuf[2] - dot(mid, mid, ((1,), (1,))))

    def second(s, carry):
        pump(s + blocks, False)
        factor_block(work, lt_out.at[1], v_out.at[1], s)
        return carry

    lax.fori_loop(0, blocks, second, 0)

    total = max((7 * (chunks - 1)) // 5 + n_col, chunks + half)
    if total > 2 * blocks:
        def rest(s, carry):
            pump(s, False)
            return carry

        lax.fori_loop(2 * blocks, total, rest, 0)

    back = [local(rbuf, r_out, loc.at[0]), local(cbuf, c_out, loc.at[1])]
    for copy in back:
        copy.start()

    def d_drain(p, carry):
        for i in range(3):
            for cond, copy in d_sends(i, p)[1]:
                pl.when(cond)(copy.wait_send)
        return carry

    lax.fori_loop(0, PIECES, d_drain, 0)

    def drain(c, carry):
        for k in range(2):
            for cond, copy in r_sends(k, c) + c_sends(k, c):
                pl.when(cond)(copy.wait_send)
        return carry

    lax.fori_loop(0, chunks, drain, 0)
    for copy in back:
        copy.wait()


def halves(x):
    hi = x.astype(jnp.bfloat16)
    lo = (x - hi.astype(jnp.float32)).astype(jnp.bfloat16)
    return hi, lo


def dot3(a, b, dims=((1,), (0,))):
    part = lambda x, y: lax.dot_general(x, y, (dims, ((), ())), preferred_element_type=jnp.float32)
    return part(a[0], b[0]) + (part(a[0], b[1]) + part(a[1], b[0]))


def update_kernel(n_row, n_col, a_ref, r_ref, c_ref, v_ref, lt_ref, mid_ref, o_ref, right):
    t = pl.program_id(0)
    row = lax.axis_index("row")
    col = lax.axis_index("col")
    n_cols = a_ref.shape[1]

    @pl.when(t == 0)
    def _():
        @pl.loop(0, n_cols // NB)
        def _(s):
            span = pl.ds(pl.multiple_of(s * NB, NB), NB)
            p0 = halves(dot3(halves(v_ref[0]), halves(c_ref[0, :, span])))
            rest = c_ref[1, :, span] - dot3(halves(mid_ref[...]), p0)
            p1 = halves(dot3(halves(v_ref[1]), halves(rest)))
            for k, (hi, lo) in enumerate((p0, p1)):
                right[pl.ds(3 * k * NB, NB), span] = hi
                right[pl.ds((3 * k + 1) * NB, NB), span] = lo
                right[pl.ds((3 * k + 2) * NB, NB), span] = hi

    g = t * n_row + row
    across = ((1,), (1,))
    q0 = dot3(halves(r_ref[0]), halves(v_ref[0]), across)
    h0, l0 = halves(q0)
    rest = r_ref[1] - dot3((h0, l0), halves(mid_ref[...]), across)
    q1 = dot3(halves(rest), halves(v_ref[1]), across)
    h1, l1 = halves(q1)
    left = jnp.concatenate([h0, h0, l0, h1, h1, l1], axis=1)
    wide = 2 * NB if n_cols % (2 * NB) == 0 else NB

    @pl.loop(0, n_cols // wide)
    def _(s):
        span = pl.ds(pl.multiple_of(s * wide, wide), wide)
        o_ref[:, span] = a_ref[:, span] - lax.dot_general(
            left, right[:, span], (((1,), (0,)), ((), ())), preferred_element_type=jnp.float32)

    @pl.when(g < 2)
    def _():
        o_ref[...] = jnp.zeros_like(o_ref)

    @pl.when(col == 0)
    def _():
        o_ref[:, :NB] = q0

        @pl.when(g == 0)
        def _():
            o_ref[:, :NB] = lt_ref[0].T

    @pl.when((col == 1) & (g > 0))
    def _():
        o_ref[:, :NB] = q1

        @pl.when(g == 1)
        def _():
            o_ref[:, :NB] = lt_ref[1].T


def body(n_row, n_col, matrix):
    n_rows, n_cols = matrix.shape
    chunks = 10
    f32 = jnp.float32
    anyspace = pl.BlockSpec(memory_space=pl.ANY)
    vmem = pl.BlockSpec(memory_space=pltpu.VMEM)
    r, c, v, lt, mid = pl.pallas_call(
        functools.partial(chain_kernel, n_row, n_col, chunks),
        out_shape=(
            jax.ShapeDtypeStruct((2, n_rows, NB), f32),
            jax.ShapeDtypeStruct((2, NB, n_cols), f32),
            jax.ShapeDtypeStruct((2, NB, NB), f32),
            jax.ShapeDtypeStruct((2, NB, NB), f32),
            jax.ShapeDtypeStruct((NB, NB), f32),
        ),
        in_specs=[anyspace],
        out_specs=(anyspace, anyspace, vmem, vmem, vmem),
        scratch_shapes=[
            pltpu.VMEM((2, n_rows, NB), f32),
            pltpu.VMEM((2, NB, n_cols), f32),
            pltpu.VMEM((3, NB, NB), f32),
            pltpu.VMEM((NB, 2 * NB), f32),
            pltpu.SemaphoreType.DMA((2, 2, chunks)),
            pltpu.SemaphoreType.DMA((2, chunks)),
            pltpu.SemaphoreType.DMA((2, 2, chunks)),
            pltpu.SemaphoreType.DMA((2, chunks)),
            pltpu.SemaphoreType.DMA((3, 5, PIECES)),
            pltpu.SemaphoreType.DMA((3, PIECES)),
            pltpu.SemaphoreType.DMA((7,)),
        ],
        compiler_params=pltpu.CompilerParams(
            collective_id=0, has_side_effects=True, vmem_limit_bytes=60 * 2**20),
        name="chain",
    )(matrix)
    whole = lambda shape: pl.BlockSpec(shape, lambda t: (0,) * len(shape), pipeline_mode=pl.Buffered(1))
    return pl.pallas_call(
        functools.partial(update_kernel, n_row, n_col),
        grid=(n_rows // NB,),
        out_shape=jax.ShapeDtypeStruct(matrix.shape, f32),
        in_specs=[
            pl.BlockSpec((NB, n_cols), lambda t: (t, 0)),
            pl.BlockSpec((2, NB, NB), lambda t: (0, t, 0)),
            whole((2, NB, n_cols)),
            whole((2, NB, NB)),
            whole((2, NB, NB)),
            whole((NB, NB)),
        ],
        out_specs=pl.BlockSpec((NB, n_cols), lambda t: (t, 0)),
        scratch_shapes=[pltpu.VMEM((6 * NB, n_cols), jnp.bfloat16)],
        compiler_params=pltpu.CompilerParams(vmem_limit_bytes=60 * 2**20),
        name="update",
    )(matrix, r, c, v, lt, mid)


def solution(mesh):
    n_row, n_col = mesh.shape["row"], mesh.shape["col"]
    return jax.shard_map(
        functools.partial(body, n_row, n_col), mesh=mesh,
        in_specs=(P("row", "col"),), out_specs=P("row", "col"), check_vma=False)
```

```python
import functools
import jax
import jax.numpy as jnp
from jax import lax
from jax.experimental import pallas as pl
from jax.experimental.pallas import tpu as pltpu
from jax.sharding import PartitionSpec as P

NB = 256
BK = 64
STEPS = 2
PIECES = 4
MESH = pl.DeviceIdType.MESH
HIGH = lax.Precision.HIGHEST


def dot(a, b, dims=((1,), (0,))):
    return lax.dot_general(a, b, (dims, ((), ())), precision=HIGH, preferred_element_type=jnp.float32)


def factor_block(work, lt_ref, v_ref, k):
    base = pl.multiple_of(k * BK, BK)
    rows = work[pl.ds(base, BK), :]
    lead = pltpu.roll(rows[:, :NB], lax.rem(NB - base, NB), 1)[:, :128]
    lane = lax.broadcasted_iota(jnp.int32, (BK, 128), 1)
    sub = lax.broadcasted_iota(jnp.int32, (BK, 128), 0)
    w = jnp.where(lane < BK, lead, jnp.where(lane == sub + BK, 1.0, 0.0))
    scale = jnp.ones((BK, 128), jnp.float32)
    for j in range(0, BK, 4):
        c = [jnp.broadcast_to(w[:, j + q:j + q + 1], (BK, 128)) for q in range(4)]
        r = [w[j + q:j + q + 1, :] for q in range(4)]
        ms, rs = [], []
        for h in (0, 2):
            c0, c1 = c[h], c[h + 1]
            r0, r1 = r[h], r[h + 1]
            i = j + h
            d, e, f = c0[i:i + 1, :], c0[i + 1:i + 2, :], c1[i + 1:i + 2, :]
            inv_d = 1.0 / d
            inv_f = d / (f * d - e * e)
            ratio = e * inv_d
            m0 = jnp.where(sub > i, c0 * inv_d, 0.0)
            m1 = jnp.where(sub > i + 1, (c1 - ratio * c0) * inv_f, 0.0)
            r1 = r1 - ratio * r0
            ms += [m0, m1]
            rs += [r0, r1]
            scale = jnp.where(sub == i, inv_d, jnp.where(sub == i + 1, inv_f, scale))
            if h == 0:
                for p in (2, 3):
                    e0 = c[p][i:i + 1, :]
                    e1 = c[p][i + 1:i + 2, :] - ratio * e0
                    r[p] = r[p] - m0[j + p:j + p + 1, :] * r0 - m1[j + p:j + p + 1, :] * r1
                    c[p] = c[p] - m0 * e0 - m1 * e1
        for m, x in zip(ms, rs):
            w = w - m * x
    w = w * jnp.sqrt(scale)
    vd = pltpu.roll(w, 128 - BK, 1)[:, :BK]
    new = dot(vd, rows)
    wide = lax.broadcasted_iota(jnp.int32, (BK, NB), 1)
    tall = lax.broadcasted_iota(jnp.int32, (BK, NB), 0)
    top = jnp.where(wide >= tall + base, new[:, :NB], 0.0)
    lt_ref[pl.ds(base, BK), :] = top
    v_ref[pl.ds(base, BK), :] = new[:, NB:]
    left = jnp.where(wide >= base + BK, top, 0.0)
    right = jnp.concatenate([top, new[:, NB:]], axis=1)
    work[...] = work[...] - dot(left, right, ((0,), (0,)))


def set_work(work, tile):
    work[:, :NB] = tile
    a = lax.broadcasted_iota(jnp.int32, (NB, NB), 0)
    b = lax.broadcasted_iota(jnp.int32, (NB, NB), 1)
    work[:, NB:] = jnp.where(a == b, 1.0, 0.0)


def pick(index, table):
    out = jnp.int32(0)
    for i, value in enumerate(table):
        out = out + jnp.where(index == i, jnp.int32(value), jnp.int32(0))
    return out


def chain_kernel(n_row, n_col, chunks, a_ref, r_out, c_out, v_out, lt_out, mid_out,
                 rbuf, cbuf, dbuf, work, r_send, r_recv, c_send, c_recv, d_send, d_recv, loc):
    row = lax.axis_index("row")
    col = lax.axis_index("col")
    n_rows = rbuf.shape[1]
    n_cols = cbuf.shape[2]
    r_step = n_rows // chunks
    c_step = n_cols // chunks
    half = n_row // 2
    order = [i ^ (i >> 1) for i in range(half)]
    orders = [order, order[:1] + order[:0:-1]]
    pair = row // 2
    core = lax.rem(row, 2)
    sibling = row + 1 - 2 * core
    nexts, hops, lasts, prevs, fwd, bwd, ring_hops = [], [], [], [], [], [], []
    for k in range(2):
        table, where, before = [0] * half, [0] * half, [0] * half
        for i, q in enumerate(orders[k]):
            table[q] = orders[k][(i + 1) % half]
            before[q] = orders[k][(i - 1) % half]
            where[q] = i
        place = pick(pair, where)
        nexts.append(2 * pick(pair, table) + k)
        prevs.append(2 * pick(pair, before) + k)
        hops.append(jnp.where(core == k, place, place + 1))
        lasts.append(place == half - 1)
        fwd.append((core == k) & (place < half // 2))
        bwd.append((core == k) & ((place == 0) | (place > half // 2 + 1)))
        near = jnp.where(place <= half // 2, place, half - place)
        ring_hops.append(jnp.where(core == k, near, near + 1))

    def remote(src, ssem, rsem, target):
        return pltpu.make_async_remote_copy(
            src_ref=src, dst_ref=src, send_sem=ssem, recv_sem=rsem, device_id=target, device_id_type=MESH)

    def local(src, dst, sem):
        return pltpu.make_async_copy(src, dst, sem)

    own = []
    for k in range(2):
        own.append((col == k, local(a_ref.at[:, pl.ds(0, NB)], rbuf.at[k], loc.at[2 * k])))
        own.append((row == k, local(a_ref.at[pl.ds(0, NB), :], cbuf.at[k], loc.at[2 * k + 1])))
    roots = ((0, 0), (1, 0), (1, 1))
    for i, (a, b) in enumerate(roots):
        own.append(((row == a) & (col == b), local(a_ref.at[pl.ds(0, NB), pl.ds(0, NB)], dbuf.at[i], loc.at[4 + i])))
    for cond, copy in own:
        pl.when(cond)(copy.start)

    barrier = pltpu.get_barrier_semaphore()
    for i in range(1, n_row):
        pl.semaphore_signal(barrier, inc=1, device_id=(lax.rem(row + i, n_row), col), device_id_type=MESH)
    for i in range(1, n_col):
        pl.semaphore_signal(barrier, inc=1, device_id=(row, lax.rem(col + i, n_col)), device_id_type=MESH)
    pl.semaphore_wait(barrier, n_row + n_col - 2)
    for cond, copy in own:
        pl.when(cond)(copy.wait)

    d_step = NB // PIECES

    def d_sends(i, p):
        a, b = roots[i]
        k = a
        tile = dbuf.at[i, pl.ds(pl.multiple_of(p * d_step, d_step), d_step), :]
        up = (row == a) & (col >= b) & (col < n_col - 1)
        down = (row == a) & (col <= b) & (col > 0)
        return tile, (
            (up, remote(tile, d_send.at[i, 0, p], d_recv.at[i, p], (row, jnp.minimum(col + 1, n_col - 1)))),
            (down, remote(tile, d_send.at[i, 1, p], d_recv.at[i, p], (row, jnp.maximum(col - 1, 0)))),
            (fwd[k], remote(tile, d_send.at[i, 2, p], d_recv.at[i, p], (nexts[k], col))),
            (bwd[k], remote(tile, d_send.at[i, 3, p], d_recv.at[i, p], (prevs[k], col))),
            (core == k, remote(tile, d_send.at[i, 4, p], d_recv.at[i, p], (sibling, col))),
        )

    def d_relay(i):
        a, b = roots[i]

        def step(p, carry):
            tile, sends = d_sends(i, p)
            pl.when((row != a) | (col != b))(
                remote(tile, d_send.at[i, 0, p], d_recv.at[i, p], (row, col)).wait_recv)
            for cond, copy in sends:
                pl.when(cond)(copy.start)
            return carry

        lax.fori_loop(0, PIECES, step, 0)

    def r_piece(k, c):
        return rbuf.at[k, pl.ds(pl.multiple_of(c * r_step, r_step), r_step), :]

    def c_piece(k, c):
        return cbuf.at[k, :, pl.ds(pl.multiple_of(c * c_step, c_step), c_step)]

    def r_sends(k, c):
        piece = r_piece(k, c)
        return (
            ((col >= k) & (col < n_col - 1),
             remote(piece, r_send.at[k, 0, c], r_recv.at[k, c], (row, jnp.minimum(col + 1, n_col - 1)))),
            ((col <= k) & (col > 0),
             remote(piece, r_send.at[k, 1, c], r_recv.at[k, c], (row, jnp.maximum(col - 1, 0)))),
        )

    def c_sends(k, c):
        piece = c_piece(k, c)
        return (
            ((core == k) & jnp.logical_not(lasts[k]),
             remote(piece, c_send.at[k, 0, c], c_recv.at[k, c], (nexts[k], col))),
            (core == k, remote(piece, c_send.at[k, 1, c], c_recv.at[k, c], (sibling, col))),
        )

    early = chunks // 2

    def r_root(k):
        def step(c, carry):
            up, down = r_sends(k, c)
            pl.when((col == k) & up[0] & ((k == 0) | (c < early)))(up[1].start)
            pl.when((col == k) & down[0])(down[1].start)
            return carry

        lax.fori_loop(0, chunks, step, 0)

    def c_root(k):
        def step(c, carry):
            for cond, copy in c_sends(k, c):
                pl.when((row == k) & cond)(copy.start)
            return carry

        lax.fori_loop(0, chunks, step, 0)

    def r_wait(k, c):
        remote(r_piece(k, c), r_send.at[k, 0, c], r_recv.at[k, c], (row, col)).wait_recv()

    def c_wait(k, c):
        remote(c_piece(k, c), c_send.at[k, 0, c], c_recv.at[k, c], (row, col)).wait_recv()

    def r_up(k, c):
        r_sends(k, c)[0][1].start()

    middle = (col >= 1) & (col < n_col - 1)

    def r_early():
        def step(c, carry):
            r_wait(1, c)
            r_up(1, c)
            return carry

        lax.fori_loop(0, early, step, 0)

    def pump(s, tiles=True):
        if tiles:
            for i in (1, 2):
                pl.when((row != roots[i][0]) & (s == ring_hops[roots[i][0]]))(lambda i=i: d_relay(i))

        def r_one(c):
            r_wait(0, c)
            r_up(0, c)

            @pl.when(c < chunks - early)
            def _():
                pl.when(col > 1)(lambda: r_wait(1, c + early))
                r_up(1, c + early)

        u = s - col
        pl.when(middle & (u >= 0) & (u < 2 * chunks) & (lax.rem(u + 2 * n_col, 2) == 0))(lambda: r_one(u // 2))
        for k in range(2):
            def c_one(c, k=k):
                c_wait(k, c)
                for cond, copy in c_sends(k, c):
                    pl.when(cond)(copy.start)

            u = s - hops[k]
            pl.when((core == k) & (row != k) & (u >= 0) & (u < 2 * chunks) & (lax.rem(u + n_row, 2) == 0))(
                lambda c_one=c_one, u=u: c_one(u // 2))

    pl.when(row > 1)(lambda: [r_root(k) for k in range(2)] and None)
    d_relay(0)
    pl.when(row == 1)(lambda: [d_relay(i) for i in (1, 2)] and None)
    pl.when(row <= 1)(lambda: [r_root(k) for k in range(2)] and None)
    for k in range(2):
        pl.when(row == k)(functools.partial(c_root, k))
    pl.when(middle & (col > 1))(r_early)

    blocks = NB // BK
    set_work(work, dbuf[0])

    def first(s, carry):
        for q in range(STEPS):
            pump(s * STEPS + q)
        factor_block(work, lt_out.at[0], v_out.at[0], s)
        return carry

    lax.fori_loop(0, blocks, first, 0)
    most = half // 2 + 2
    if most > blocks * STEPS:
        def tiles_rest(s, carry):
            for i in (1, 2):
                pl.when((row != roots[i][0]) & (s == ring_hops[roots[i][0]]))(lambda i=i: d_relay(i))
            return carry

        lax.fori_loop(blocks * STEPS, most, tiles_rest, 0)
    mid = dot(dbuf[1], v_out[0], ((1,), (1,)))
    mid_out[...] = mid
    set_work(work, dbuf[2] - dot(mid, mid, ((1,), (1,))))

    def second(s, carry):
        for q in range(STEPS):
            pump((s + blocks) * STEPS + q, False)
        factor_block(work, lt_out.at[1], v_out.at[1], s)
        return carry

    lax.fori_loop(0, blocks, second, 0)

    total = 2 * chunks - 1 + max(n_col - 1, half)
    done = 2 * blocks * STEPS
    if total > done:
        def rest(s, carry):
            pump(s, False)
            return carry

        lax.fori_loop(done, total, rest, 0)

    def ends(c, carry):
        pl.when(col == n_col - 1)(lambda: r_wait(0, c))
        pl.when((col == 0) | ((col == n_col - 1) & (col > 1)))(lambda: r_wait(1, c))
        for k in range(2):
            pl.when(core != k)(lambda k=k: c_wait(k, c))
        return carry

    lax.fori_loop(0, chunks, ends, 0)

    back = [local(rbuf, r_out, loc.at[0]), local(cbuf, c_out, loc.at[1])]
    for copy in back:
        copy.start()

    def d_drain(p, carry):
        for i in range(3):
            for cond, copy in d_sends(i, p)[1]:
                pl.when(cond)(copy.wait_send)
        return carry

    lax.fori_loop(0, PIECES, d_drain, 0)

    def drain(c, carry):
        for k in range(2):
            for cond, copy in r_sends(k, c) + c_sends(k, c):
                pl.when(cond)(copy.wait_send)
        return carry

    lax.fori_loop(0, chunks, drain, 0)
    for copy in back:
        copy.wait()


def halves(x):
    hi = x.astype(jnp.bfloat16)
    lo = (x - hi.astype(jnp.float32)).astype(jnp.bfloat16)
    return hi, lo


def dot3(a, b, dims=((1,), (0,))):
    part = lambda x, y: lax.dot_general(x, y, (dims, ((), ())), preferred_element_type=jnp.float32)
    return part(a[0], b[0]) + (part(a[0], b[1]) + part(a[1], b[0]))


def update_kernel(n_row, n_col, a_ref, r_ref, c_ref, v_ref, lt_ref, mid_ref, o_ref, right):
    t = pl.program_id(0)
    row = lax.axis_index("row")
    col = lax.axis_index("col")
    n_cols = a_ref.shape[1]

    @pl.when(t == 0)
    def _():
        @pl.loop(0, n_cols // NB)
        def _(s):
            span = pl.ds(pl.multiple_of(s * NB, NB), NB)
            p0 = halves(dot3(halves(v_ref[0]), halves(c_ref[0, :, span])))
            rest = c_ref[1, :, span] - dot3(halves(mid_ref[...]), p0)
            p1 = halves(dot3(halves(v_ref[1]), halves(rest)))
            for k, (hi, lo) in enumerate((p0, p1)):
                right[pl.ds(3 * k * NB, NB), span] = hi
                right[pl.ds((3 * k + 1) * NB, NB), span] = lo
                right[pl.ds((3 * k + 2) * NB, NB), span] = hi

    g = t * n_row + row
    across = ((1,), (1,))
    q0 = dot3(halves(r_ref[0]), halves(v_ref[0]), across)
    h0, l0 = halves(q0)
    rest = r_ref[1] - dot3((h0, l0), halves(mid_ref[...]), across)
    q1 = dot3(halves(rest), halves(v_ref[1]), across)
    h1, l1 = halves(q1)
    left = jnp.concatenate([h0, h0, l0, h1, h1, l1], axis=1)
    wide = 2 * NB if n_cols % (2 * NB) == 0 else NB

    @pl.loop(0, n_cols // wide)
    def _(s):
        span = pl.ds(pl.multiple_of(s * wide, wide), wide)
        o_ref[:, span] = a_ref[:, span] - lax.dot_general(
            left, right[:, span], (((1,), (0,)), ((), ())), preferred_element_type=jnp.float32)

    @pl.when(g < 2)
    def _():
        o_ref[...] = jnp.zeros_like(o_ref)

    @pl.when(col == 0)
    def _():
        o_ref[:, :NB] = q0

        @pl.when(g == 0)
        def _():
            o_ref[:, :NB] = lt_ref[0].T

    @pl.when((col == 1) & (g > 0))
    def _():
        o_ref[:, :NB] = q1

        @pl.when(g == 1)
        def _():
            o_ref[:, :NB] = lt_ref[1].T


def body(n_row, n_col, matrix):
    n_rows, n_cols = matrix.shape
    chunks = 10
    f32 = jnp.float32
    anyspace = pl.BlockSpec(memory_space=pl.ANY)
    vmem = pl.BlockSpec(memory_space=pltpu.VMEM)
    r, c, v, lt, mid = pl.pallas_call(
        functools.partial(chain_kernel, n_row, n_col, chunks),
        out_shape=(
            jax.ShapeDtypeStruct((2, n_rows, NB), f32),
            jax.ShapeDtypeStruct((2, NB, n_cols), f32),
            jax.ShapeDtypeStruct((2, NB, NB), f32),
            jax.ShapeDtypeStruct((2, NB, NB), f32),
            jax.ShapeDtypeStruct((NB, NB), f32),
        ),
        in_specs=[anyspace],
        out_specs=(anyspace, anyspace, vmem, vmem, vmem),
        scratch_shapes=[
            pltpu.VMEM((2, n_rows, NB), f32),
            pltpu.VMEM((2, NB, n_cols), f32),
            pltpu.VMEM((3, NB, NB), f32),
            pltpu.VMEM((NB, 2 * NB), f32),
            pltpu.SemaphoreType.DMA((2, 2, chunks)),
            pltpu.SemaphoreType.DMA((2, chunks)),
            pltpu.SemaphoreType.DMA((2, 2, chunks)),
            pltpu.SemaphoreType.DMA((2, chunks)),
            pltpu.SemaphoreType.DMA((3, 5, PIECES)),
            pltpu.SemaphoreType.DMA((3, PIECES)),
            pltpu.SemaphoreType.DMA((7,)),
        ],
        compiler_params=pltpu.CompilerParams(
            collective_id=0, has_side_effects=True, vmem_limit_bytes=60 * 2**20),
        name="chain",
    )(matrix)
    whole = lambda shape: pl.BlockSpec(shape, lambda t: (0,) * len(shape), pipeline_mode=pl.Buffered(1))
    return pl.pallas_call(
        functools.partial(update_kernel, n_row, n_col),
        grid=(n_rows // NB,),
        out_shape=jax.ShapeDtypeStruct(matrix.shape, f32),
        in_specs=[
            pl.BlockSpec((NB, n_cols), lambda t: (t, 0)),
            pl.BlockSpec((2, NB, NB), lambda t: (0, t, 0)),
            whole((2, NB, n_cols)),
            whole((2, NB, NB)),
            whole((2, NB, NB)),
            whole((NB, NB)),
        ],
        out_specs=pl.BlockSpec((NB, n_cols), lambda t: (t, 0)),
        scratch_shapes=[pltpu.VMEM((6 * NB, n_cols), jnp.bfloat16)],
        compiler_params=pltpu.CompilerParams(vmem_limit_bytes=60 * 2**20),
        name="update",
    )(matrix, r, c, v, lt, mid)


def solution(mesh):
    n_row, n_col = mesh.shape["row"], mesh.shape["col"]
    return jax.shard_map(
        functools.partial(body, n_row, n_col), mesh=mesh,
        in_specs=(P("row", "col"),), out_specs=P("row", "col"), check_vma=False)
```

```python
import functools
import jax
import jax.numpy as jnp
from jax import lax
from jax.experimental import pallas as pl
from jax.experimental.pallas import tpu as pltpu
from jax.sharding import PartitionSpec as P

NB = 256
BK = 64
STEPS = 2
PIECES = 4
MESH = pl.DeviceIdType.MESH
HIGH = lax.Precision.HIGHEST


def dot(a, b, dims=((1,), (0,))):
    return lax.dot_general(a, b, (dims, ((), ())), precision=HIGH, preferred_element_type=jnp.float32)


def factor_block(work, lt_ref, v_ref, k):
    base = pl.multiple_of(k * BK, BK)
    rows = work[pl.ds(base, BK), :]
    lead = pltpu.roll(rows[:, :NB], lax.rem(NB - base, NB), 1)[:, :128]
    lane = lax.broadcasted_iota(jnp.int32, (BK, 128), 1)
    sub = lax.broadcasted_iota(jnp.int32, (BK, 128), 0)
    w = jnp.where(lane < BK, lead, jnp.where(lane == sub + BK, 1.0, 0.0))
    scale = jnp.ones((BK, 128), jnp.float32)
    for j in range(0, BK, 4):
        c = [jnp.broadcast_to(w[:, j + q:j + q + 1], (BK, 128)) for q in range(4)]
        r = [w[j + q:j + q + 1, :] for q in range(4)]
        ms, rs = [], []
        for h in (0, 2):
            c0, c1 = c[h], c[h + 1]
            r0, r1 = r[h], r[h + 1]
            i = j + h
            d, e, f = c0[i:i + 1, :], c0[i + 1:i + 2, :], c1[i + 1:i + 2, :]
            inv_d = 1.0 / d
            inv_f = d / (f * d - e * e)
            ratio = e * inv_d
            m0 = jnp.where(sub > i, c0 * inv_d, 0.0)
            m1 = jnp.where(sub > i + 1, (c1 - ratio * c0) * inv_f, 0.0)
            r1 = r1 - ratio * r0
            ms += [m0, m1]
            rs += [r0, r1]
            scale = jnp.where(sub == i, inv_d, jnp.where(sub == i + 1, inv_f, scale))
            if h == 0:
                for p in (2, 3):
                    e0 = c[p][i:i + 1, :]
                    e1 = c[p][i + 1:i + 2, :] - ratio * e0
                    r[p] = r[p] - m0[j + p:j + p + 1, :] * r0 - m1[j + p:j + p + 1, :] * r1
                    c[p] = c[p] - m0 * e0 - m1 * e1
        for m, x in zip(ms, rs):
            w = w - m * x
    w = w * jnp.sqrt(scale)
    vd = pltpu.roll(w, 128 - BK, 1)[:, :BK]
    new = dot(vd, rows)
    wide = lax.broadcasted_iota(jnp.int32, (BK, NB), 1)
    tall = lax.broadcasted_iota(jnp.int32, (BK, NB), 0)
    top = jnp.where(wide >= tall + base, new[:, :NB], 0.0)
    lt_ref[pl.ds(base, BK), :] = top
    v_ref[pl.ds(base, BK), :] = new[:, NB:]
    left = jnp.where(wide >= base + BK, top, 0.0)
    right = jnp.concatenate([top, new[:, NB:]], axis=1)
    work[...] = work[...] - dot(left, right, ((0,), (0,)))


def set_work(work, tile):
    work[:, :NB] = tile
    a = lax.broadcasted_iota(jnp.int32, (NB, NB), 0)
    b = lax.broadcasted_iota(jnp.int32, (NB, NB), 1)
    work[:, NB:] = jnp.where(a == b, 1.0, 0.0)


def pick(index, table):
    out = jnp.int32(0)
    for i, value in enumerate(table):
        out = out + jnp.where(index == i, jnp.int32(value), jnp.int32(0))
    return out


def chain_kernel(n_row, n_col, chunks, a_ref, r_out, c_out, v_out, lt_out, mid_out,
                 rbuf, cbuf, dbuf, work, r_send, r_recv, c_send, c_recv, d_send, d_recv, loc, right):
    row = lax.axis_index("row")
    col = lax.axis_index("col")
    n_rows = rbuf.shape[1]
    n_cols = cbuf.shape[2]
    r_step = n_rows // chunks
    c_step = n_cols // chunks
    half = n_row // 2
    order = [i ^ (i >> 1) for i in range(half)]
    orders = [order, order[:1] + order[:0:-1]]
    pair = row // 2
    core = lax.rem(row, 2)
    sibling = row + 1 - 2 * core
    nexts, hops, lasts, prevs, fwd, bwd, ring_hops = [], [], [], [], [], [], []
    for k in range(2):
        table, where, before = [0] * half, [0] * half, [0] * half
        for i, q in enumerate(orders[k]):
            table[q] = orders[k][(i + 1) % half]
            before[q] = orders[k][(i - 1) % half]
            where[q] = i
        place = pick(pair, where)
        nexts.append(2 * pick(pair, table) + k)
        prevs.append(2 * pick(pair, before) + k)
        hops.append(jnp.where(core == k, place, place + 1))
        lasts.append(place == half - 1)
        fwd.append((core == k) & (place < half // 2))
        bwd.append((core == k) & ((place == 0) | (place > half // 2 + 1)))
        near = jnp.where(place <= half // 2, place, half - place)
        ring_hops.append(jnp.where(core == k, near, near + 1))

    def remote(src, ssem, rsem, target):
        return pltpu.make_async_remote_copy(
            src_ref=src, dst_ref=src, send_sem=ssem, recv_sem=rsem, device_id=target, device_id_type=MESH)

    def local(src, dst, sem):
        return pltpu.make_async_copy(src, dst, sem)

    own = []
    for k in range(2):
        own.append((col == k, local(a_ref.at[:, pl.ds(0, NB)], rbuf.at[k], loc.at[2 * k])))
        own.append((row == k, local(a_ref.at[pl.ds(0, NB), :], cbuf.at[k], loc.at[2 * k + 1])))
    roots = ((0, 0), (1, 0), (1, 1))
    for i, (a, b) in enumerate(roots):
        own.append(((row == a) & (col == b), local(a_ref.at[pl.ds(0, NB), pl.ds(0, NB)], dbuf.at[i], loc.at[4 + i])))
    for cond, copy in own:
        pl.when(cond)(copy.start)

    barrier = pltpu.get_barrier_semaphore()
    for i in range(1, n_row):
        pl.semaphore_signal(barrier, inc=1, device_id=(lax.rem(row + i, n_row), col), device_id_type=MESH)
    for i in range(1, n_col):
        pl.semaphore_signal(barrier, inc=1, device_id=(row, lax.rem(col + i, n_col)), device_id_type=MESH)
    pl.semaphore_wait(barrier, n_row + n_col - 2)
    for cond, copy in own:
        pl.when(cond)(copy.wait)

    d_step = NB // PIECES

    def d_sends(i, p):
        a, b = roots[i]
        k = a
        tile = dbuf.at[i, pl.ds(pl.multiple_of(p * d_step, d_step), d_step), :]
        up = (row == a) & (col >= b) & (col < n_col - 1)
        down = (row == a) & (col <= b) & (col > 0)
        return tile, (
            (up, remote(tile, d_send.at[i, 0, p], d_recv.at[i, p], (row, jnp.minimum(col + 1, n_col - 1)))),
            (down, remote(tile, d_send.at[i, 1, p], d_recv.at[i, p], (row, jnp.maximum(col - 1, 0)))),
            (fwd[k], remote(tile, d_send.at[i, 2, p], d_recv.at[i, p], (nexts[k], col))),
            (bwd[k], remote(tile, d_send.at[i, 3, p], d_recv.at[i, p], (prevs[k], col))),
            (core == k, remote(tile, d_send.at[i, 4, p], d_recv.at[i, p], (sibling, col))),
        )

    def d_relay(i):
        a, b = roots[i]

        def step(p, carry):
            tile, sends = d_sends(i, p)
            pl.when((row != a) | (col != b))(
                remote(tile, d_send.at[i, 0, p], d_recv.at[i, p], (row, col)).wait_recv)
            for cond, copy in sends:
                pl.when(cond)(copy.start)
            return carry

        lax.fori_loop(0, PIECES, step, 0)

    def r_piece(k, c):
        return rbuf.at[k, pl.ds(pl.multiple_of(c * r_step, r_step), r_step), :]

    def c_piece(k, c):
        return cbuf.at[k, :, pl.ds(pl.multiple_of(c * c_step, c_step), c_step)]

    def r_sends(k, c):
        piece = r_piece(k, c)
        return (
            ((col >= k) & (col < n_col - 1),
             remote(piece, r_send.at[k, 0, c], r_recv.at[k, c], (row, jnp.minimum(col + 1, n_col - 1)))),
            ((col <= k) & (col > 0),
             remote(piece, r_send.at[k, 1, c], r_recv.at[k, c], (row, jnp.maximum(col - 1, 0)))),
        )

    def c_sends(k, c):
        piece = c_piece(k, c)
        return (
            ((core == k) & jnp.logical_not(lasts[k]),
             remote(piece, c_send.at[k, 0, c], c_recv.at[k, c], (nexts[k], col))),
            (core == k, remote(piece, c_send.at[k, 1, c], c_recv.at[k, c], (sibling, col))),
        )

    early = chunks // 2

    def r_root(k):
        def step(c, carry):
            up, down = r_sends(k, c)
            pl.when((col == k) & up[0] & ((k == 0) | (c < early)))(up[1].start)
            pl.when((col == k) & down[0])(down[1].start)
            return carry

        lax.fori_loop(0, chunks, step, 0)

    def c_root(k):
        def step(c, carry):
            for cond, copy in c_sends(k, c):
                pl.when((row == k) & cond)(copy.start)
            return carry

        lax.fori_loop(0, chunks, step, 0)

    def r_wait(k, c):
        remote(r_piece(k, c), r_send.at[k, 0, c], r_recv.at[k, c], (row, col)).wait_recv()

    def c_wait(k, c):
        remote(c_piece(k, c), c_send.at[k, 0, c], c_recv.at[k, c], (row, col)).wait_recv()

    def r_up(k, c):
        r_sends(k, c)[0][1].start()

    middle = (col >= 1) & (col < n_col - 1)

    def r_early():
        def step(c, carry):
            r_wait(1, c)
            r_up(1, c)
            return carry

        lax.fori_loop(0, early, step, 0)

    def pump(s, tiles=True):
        if tiles:
            for i in (1, 2):
                pl.when((row != roots[i][0]) & (s == ring_hops[roots[i][0]]))(lambda i=i: d_relay(i))

        def r_one(c):
            r_wait(0, c)
            r_up(0, c)

            @pl.when(c < chunks - early)
            def _():
                pl.when(col > 1)(lambda: r_wait(1, c + early))
                r_up(1, c + early)

        u = s - col
        pl.when(middle & (u >= 0) & (u < 2 * chunks) & (lax.rem(u + 2 * n_col, 2) == 0))(lambda: r_one(u // 2))
        for k in range(2):
            def c_one(c, k=k):
                c_wait(k, c)
                for cond, copy in c_sends(k, c):
                    pl.when(cond)(copy.start)

            u = s - hops[k]
            pl.when((core == k) & (row != k) & (u >= 0) & (u < 2 * chunks) & (lax.rem(u + n_row, 2) == 0))(
                lambda c_one=c_one, u=u: c_one(u // 2))

    pl.when(row > 1)(lambda: [r_root(k) for k in range(2)] and None)
    pl.when((row > 1) & middle & (col > 1))(r_early)
    d_relay(0)
    pl.when(row == 1)(lambda: [d_relay(i) for i in (1, 2)] and None)
    pl.when(row <= 1)(lambda: [r_root(k) for k in range(2)] and None)
    for k in range(2):
        pl.when(row == k)(functools.partial(c_root, k))
    pl.when((row <= 1) & middle & (col > 1))(r_early)

    blocks = NB // BK
    set_work(work, dbuf[0])

    def first(s, carry):
        for q in range(STEPS):
            pump(s * STEPS + q)
        factor_block(work, lt_out.at[0], v_out.at[0], s)
        return carry

    lax.fori_loop(0, blocks, first, 0)
    most = half // 2 + 2
    if most > blocks * STEPS:
        def tiles_rest(s, carry):
            for i in (1, 2):
                pl.when((row != roots[i][0]) & (s == ring_hops[roots[i][0]]))(lambda i=i: d_relay(i))
            return carry

        lax.fori_loop(blocks * STEPS, most, tiles_rest, 0)
    mid = dot(dbuf[1], v_out[0], ((1,), (1,)))
    mid_out[...] = mid
    set_work(work, dbuf[2] - dot(mid, mid, ((1,), (1,))))

    def second(s, carry):
        for q in range(STEPS):
            pump((s + blocks) * STEPS + q, False)
        factor_block(work, lt_out.at[1], v_out.at[1], s)
        return carry

    lax.fori_loop(0, blocks, second, 0)

    total = 2 * chunks - 1 + max(n_col - 1, half)
    done = 2 * blocks * STEPS
    ahead = max(done, total - chunks) if chunks - 1 + half > done else done

    def rest(s, carry):
        pump(s, False)
        return carry

    if ahead > done:
        lax.fori_loop(done, ahead, rest, 0)

    def panels(c, carry):
        pump(ahead + c, False)
        for k in range(2):
            pl.when(core != k)(lambda k=k: c_wait(k, c))
        span = pl.ds(pl.multiple_of(c * c_step, c_step), c_step)
        p0 = halves(dot3(halves(v_out[0]), halves(cbuf[0, :, span])))
        left = cbuf[1, :, span] - dot3(halves(mid_out[...]), p0)
        p1 = halves(dot3(halves(v_out[1]), halves(left)))
        for k, (hi, lo) in enumerate((p0, p1)):
            right[pl.ds(3 * k * NB, NB), span] = hi
            right[pl.ds((3 * k + 1) * NB, NB), span] = lo
            right[pl.ds((3 * k + 2) * NB, NB), span] = hi
        return carry

    lax.fori_loop(0, chunks, panels, 0)
    if total > ahead + chunks:
        lax.fori_loop(ahead + chunks, total, rest, 0)
    c_back = local(right, c_out, loc.at[1])
    c_back.start()

    def ends(c, carry):
        pl.when(col == n_col - 1)(lambda: r_wait(0, c))
        pl.when((col == 0) | ((col == n_col - 1) & (col > 1)))(lambda: r_wait(1, c))
        return carry

    lax.fori_loop(0, chunks, ends, 0)

    back = [local(rbuf, r_out, loc.at[0])]
    for copy in back:
        copy.start()
    back.append(c_back)

    def d_drain(p, carry):
        for i in range(3):
            for cond, copy in d_sends(i, p)[1]:
                pl.when(cond)(copy.wait_send)
        return carry

    lax.fori_loop(0, PIECES, d_drain, 0)

    def drain(c, carry):
        for k in range(2):
            for cond, copy in r_sends(k, c) + c_sends(k, c):
                pl.when(cond)(copy.wait_send)
        return carry

    lax.fori_loop(0, chunks, drain, 0)
    for copy in back:
        copy.wait()


def halves(x):
    hi = x.astype(jnp.bfloat16)
    lo = (x - hi.astype(jnp.float32)).astype(jnp.bfloat16)
    return hi, lo


def dot3(a, b, dims=((1,), (0,))):
    part = lambda x, y: lax.dot_general(x, y, (dims, ((), ())), preferred_element_type=jnp.float32)
    return part(a[0], b[0]) + (part(a[0], b[1]) + part(a[1], b[0]))


def update_kernel(n_row, n_col, a_ref, r_ref, right, v_ref, lt_ref, mid_ref, o_ref):
    t = pl.program_id(0)
    row = lax.axis_index("row")
    col = lax.axis_index("col")
    n_cols = a_ref.shape[1]

    g = t * n_row + row
    across = ((1,), (1,))
    q0 = dot3(halves(r_ref[0]), halves(v_ref[0]), across)
    h0, l0 = halves(q0)
    rest = r_ref[1] - dot3((h0, l0), halves(mid_ref[...]), across)
    q1 = dot3(halves(rest), halves(v_ref[1]), across)
    h1, l1 = halves(q1)
    left = jnp.concatenate([h0, h0, l0, h1, h1, l1], axis=1)
    wide = 2 * NB if n_cols % (2 * NB) == 0 else NB

    @pl.loop(0, n_cols // wide)
    def _(s):
        span = pl.ds(pl.multiple_of(s * wide, wide), wide)
        o_ref[:, span] = a_ref[:, span] - lax.dot_general(
            left, right[:, span], (((1,), (0,)), ((), ())), preferred_element_type=jnp.float32)

    @pl.when(g < 2)
    def _():
        o_ref[...] = jnp.zeros_like(o_ref)

    @pl.when(col == 0)
    def _():
        o_ref[:, :NB] = q0

        @pl.when(g == 0)
        def _():
            o_ref[:, :NB] = lt_ref[0].T

    @pl.when((col == 1) & (g > 0))
    def _():
        o_ref[:, :NB] = q1

        @pl.when(g == 1)
        def _():
            o_ref[:, :NB] = lt_ref[1].T


def body(n_row, n_col, matrix):
    n_rows, n_cols = matrix.shape
    chunks = 10
    f32 = jnp.float32
    anyspace = pl.BlockSpec(memory_space=pl.ANY)
    vmem = pl.BlockSpec(memory_space=pltpu.VMEM)
    r, c, v, lt, mid = pl.pallas_call(
        functools.partial(chain_kernel, n_row, n_col, chunks),
        out_shape=(
            jax.ShapeDtypeStruct((2, n_rows, NB), f32),
            jax.ShapeDtypeStruct((6 * NB, n_cols), jnp.bfloat16),
            jax.ShapeDtypeStruct((2, NB, NB), f32),
            jax.ShapeDtypeStruct((2, NB, NB), f32),
            jax.ShapeDtypeStruct((NB, NB), f32),
        ),
        in_specs=[anyspace],
        out_specs=(anyspace, anyspace, vmem, vmem, vmem),
        scratch_shapes=[
            pltpu.VMEM((2, n_rows, NB), f32),
            pltpu.VMEM((2, NB, n_cols), f32),
            pltpu.VMEM((3, NB, NB), f32),
            pltpu.VMEM((NB, 2 * NB), f32),
            pltpu.SemaphoreType.DMA((2, 2, chunks)),
            pltpu.SemaphoreType.DMA((2, chunks)),
            pltpu.SemaphoreType.DMA((2, 2, chunks)),
            pltpu.SemaphoreType.DMA((2, chunks)),
            pltpu.SemaphoreType.DMA((3, 5, PIECES)),
            pltpu.SemaphoreType.DMA((3, PIECES)),
            pltpu.SemaphoreType.DMA((7,)),
            pltpu.VMEM((6 * NB, n_cols), jnp.bfloat16),
        ],
        compiler_params=pltpu.CompilerParams(
            collective_id=0, has_side_effects=True, vmem_limit_bytes=60 * 2**20),
        name="chain",
    )(matrix)
    whole = lambda shape: pl.BlockSpec(shape, lambda t: (0,) * len(shape), pipeline_mode=pl.Buffered(1))
    return pl.pallas_call(
        functools.partial(update_kernel, n_row, n_col),
        grid=(n_rows // NB,),
        out_shape=jax.ShapeDtypeStruct(matrix.shape, f32),
        in_specs=[
            pl.BlockSpec((NB, n_cols), lambda t: (t, 0)),
            pl.BlockSpec((2, NB, NB), lambda t: (0, t, 0)),
            whole((6 * NB, n_cols)),
            whole((2, NB, NB)),
            whole((2, NB, NB)),
            whole((NB, NB)),
        ],
        out_specs=pl.BlockSpec((NB, n_cols), lambda t: (t, 0)),
        compiler_params=pltpu.CompilerParams(vmem_limit_bytes=60 * 2**20),
        name="update",
    )(matrix, r, c, v, lt, mid)


def solution(mesh):
    n_row, n_col = mesh.shape["row"], mesh.shape["col"]
    return jax.shard_map(
        functools.partial(body, n_row, n_col), mesh=mesh,
        in_specs=(P("row", "col"),), out_specs=P("row", "col"), check_vma=False)
```

```python
import functools
import jax
import jax.numpy as jnp
from jax import lax
from jax.experimental import pallas as pl
from jax.experimental.pallas import tpu as pltpu
from jax.sharding import PartitionSpec as P

NB = 256
BK = 64
STEPS = 2
PIECES = 4
MESH = pl.DeviceIdType.MESH
HIGH = lax.Precision.HIGHEST


def dot(a, b, dims=((1,), (0,))):
    return lax.dot_general(a, b, (dims, ((), ())), precision=HIGH, preferred_element_type=jnp.float32)


def factor_block(work, lt_ref, v_ref, k):
    base = pl.multiple_of(k * BK, BK)
    rows = work[pl.ds(base, BK), :]
    lead = pltpu.roll(rows[:, :NB], lax.rem(NB - base, NB), 1)[:, :128]
    lane = lax.broadcasted_iota(jnp.int32, (BK, 128), 1)
    sub = lax.broadcasted_iota(jnp.int32, (BK, 128), 0)
    w = jnp.where(lane < BK, lead, jnp.where(lane == sub + BK, 1.0, 0.0))
    scale = jnp.ones((BK, 128), jnp.float32)
    for j in range(0, BK, 4):
        c = [jnp.broadcast_to(w[:, j + q:j + q + 1], (BK, 128)) for q in range(4)]
        r = [w[j + q:j + q + 1, :] for q in range(4)]
        ms, rs = [], []
        for h in (0, 2):
            c0, c1 = c[h], c[h + 1]
            r0, r1 = r[h], r[h + 1]
            i = j + h
            d, e, f = c0[i:i + 1, :], c0[i + 1:i + 2, :], c1[i + 1:i + 2, :]
            inv_d = 1.0 / d
            inv_f = d / (f * d - e * e)
            ratio = e * inv_d
            m0 = jnp.where(sub > i, c0 * inv_d, 0.0)
            m1 = jnp.where(sub > i + 1, (c1 - ratio * c0) * inv_f, 0.0)
            r1 = r1 - ratio * r0
            ms += [m0, m1]
            rs += [r0, r1]
            scale = jnp.where(sub == i, inv_d, jnp.where(sub == i + 1, inv_f, scale))
            if h == 0:
                for p in (2, 3):
                    e0 = c[p][i:i + 1, :]
                    e1 = c[p][i + 1:i + 2, :] - ratio * e0
                    r[p] = r[p] - m0[j + p:j + p + 1, :] * r0 - m1[j + p:j + p + 1, :] * r1
                    c[p] = c[p] - m0 * e0 - m1 * e1
        for m, x in zip(ms, rs):
            w = w - m * x
    w = w * jnp.sqrt(scale)
    vd = pltpu.roll(w, 128 - BK, 1)[:, :BK]
    new = dot(vd, rows)
    wide = lax.broadcasted_iota(jnp.int32, (BK, NB), 1)
    tall = lax.broadcasted_iota(jnp.int32, (BK, NB), 0)
    top = jnp.where(wide >= tall + base, new[:, :NB], 0.0)
    lt_ref[pl.ds(base, BK), :] = top
    v_ref[pl.ds(base, BK), :] = new[:, NB:]
    left = jnp.where(wide >= base + BK, top, 0.0)
    right = jnp.concatenate([top, new[:, NB:]], axis=1)
    work[...] = work[...] - dot(left, right, ((0,), (0,)))


def set_work(work, tile):
    work[:, :NB] = tile
    a = lax.broadcasted_iota(jnp.int32, (NB, NB), 0)
    b = lax.broadcasted_iota(jnp.int32, (NB, NB), 1)
    work[:, NB:] = jnp.where(a == b, 1.0, 0.0)


def pick(index, table):
    out = jnp.int32(0)
    for i, value in enumerate(table):
        out = out + jnp.where(index == i, jnp.int32(value), jnp.int32(0))
    return out


def chain_kernel(n_row, n_col, chunks, a_ref, r_out, c_out, v_out, lt_out, mid_out,
                 rbuf, cbuf, dbuf, work, r_send, r_recv, c_send, c_recv, d_send, d_recv, loc, right):
    row = lax.axis_index("row")
    col = lax.axis_index("col")
    n_rows = rbuf.shape[1]
    n_cols = cbuf.shape[2]
    r_step = n_rows // chunks
    c_step = n_cols // chunks
    half = n_row // 2
    order = [i ^ (i >> 1) for i in range(half)]
    orders = [order, order[:1] + order[:0:-1]]
    pair = row // 2
    core = lax.rem(row, 2)
    sibling = row + 1 - 2 * core
    nexts, hops, lasts, prevs, fwd, bwd, ring_hops = [], [], [], [], [], [], []
    for k in range(2):
        table, where, before = [0] * half, [0] * half, [0] * half
        for i, q in enumerate(orders[k]):
            table[q] = orders[k][(i + 1) % half]
            before[q] = orders[k][(i - 1) % half]
            where[q] = i
        place = pick(pair, where)
        nexts.append(2 * pick(pair, table) + k)
        prevs.append(2 * pick(pair, before) + k)
        hops.append(jnp.where(core == k, place, place + 1))
        lasts.append(place == half - 1)
        fwd.append((core == k) & (place < half // 2))
        bwd.append((core == k) & ((place == 0) | (place > half // 2 + 1)))
        near = jnp.where(place <= half // 2, place, half - place)
        ring_hops.append(jnp.where(core == k, near, near + 1))

    def remote(src, ssem, rsem, target):
        return pltpu.make_async_remote_copy(
            src_ref=src, dst_ref=src, send_sem=ssem, recv_sem=rsem, device_id=target, device_id_type=MESH)

    def local(src, dst, sem):
        return pltpu.make_async_copy(src, dst, sem)

    own = []
    for k in range(2):
        own.append((col == k, local(a_ref.at[:, pl.ds(0, NB)], rbuf.at[k], loc.at[2 * k])))
        own.append((row == k, local(a_ref.at[pl.ds(0, NB), :], cbuf.at[k], loc.at[2 * k + 1])))
    roots = ((0, 0), (1, 0), (1, 1))
    for i, (a, b) in enumerate(roots):
        own.append(((row == a) & (col == b), local(a_ref.at[pl.ds(0, NB), pl.ds(0, NB)], dbuf.at[i], loc.at[4 + i])))
    for cond, copy in own:
        pl.when(cond)(copy.start)

    barrier = pltpu.get_barrier_semaphore()
    for i in range(1, n_row):
        pl.semaphore_signal(barrier, inc=1, device_id=(lax.rem(row + i, n_row), col), device_id_type=MESH)
    for i in range(1, n_col):
        pl.semaphore_signal(barrier, inc=1, device_id=(row, lax.rem(col + i, n_col)), device_id_type=MESH)
    pl.semaphore_wait(barrier, n_row + n_col - 2)
    for cond, copy in own:
        pl.when(cond)(copy.wait)

    d_step = NB // PIECES

    def d_sends(i, p):
        a, b = roots[i]
        k = a
        tile = dbuf.at[i, pl.ds(pl.multiple_of(p * d_step, d_step), d_step), :]
        up = (row == a) & (col >= b) & (col < n_col - 1)
        down = (row == a) & (col <= b) & (col > 0)
        return tile, (
            (up, remote(tile, d_send.at[i, 0, p], d_recv.at[i, p], (row, jnp.minimum(col + 1, n_col - 1)))),
            (down, remote(tile, d_send.at[i, 1, p], d_recv.at[i, p], (row, jnp.maximum(col - 1, 0)))),
            (fwd[k], remote(tile, d_send.at[i, 2, p], d_recv.at[i, p], (nexts[k], col))),
            (bwd[k], remote(tile, d_send.at[i, 3, p], d_recv.at[i, p], (prevs[k], col))),
            (core == k, remote(tile, d_send.at[i, 4, p], d_recv.at[i, p], (sibling, col))),
        )

    def d_relay(i):
        a, b = roots[i]

        def step(p, carry):
            tile, sends = d_sends(i, p)
            pl.when((row != a) | (col != b))(
                remote(tile, d_send.at[i, 0, p], d_recv.at[i, p], (row, col)).wait_recv)
            for cond, copy in sends:
                pl.when(cond)(copy.start)
            return carry

        lax.fori_loop(0, PIECES, step, 0)

    def r_piece(k, c):
        return rbuf.at[k, pl.ds(pl.multiple_of(c * r_step, r_step), r_step), :]

    def c_piece(k, c):
        return cbuf.at[k, :, pl.ds(pl.multiple_of(c * c_step, c_step), c_step)]

    def keep(c):
        return (row > 1) | (c >= NB // r_step)

    def r_sends(k, c):
        piece = r_piece(k, c)
        return (
            ((col >= k) & (col < n_col - 1) & keep(c),
             remote(piece, r_send.at[k, 0, c], r_recv.at[k, c], (row, jnp.minimum(col + 1, n_col - 1)))),
            ((col <= k) & (col > 0) & keep(c),
             remote(piece, r_send.at[k, 1, c], r_recv.at[k, c], (row, jnp.maximum(col - 1, 0)))),
        )

    def c_sends(k, c):
        piece = c_piece(k, c)
        return (
            ((core == k) & jnp.logical_not(lasts[k]),
             remote(piece, c_send.at[k, 0, c], c_recv.at[k, c], (nexts[k], col))),
            (core == k, remote(piece, c_send.at[k, 1, c], c_recv.at[k, c], (sibling, col))),
        )

    early = chunks // 2

    def r_root(k):
        def step(c, carry):
            up, down = r_sends(k, c)
            pl.when((col == k) & up[0] & ((k == 0) | (c < early)))(up[1].start)
            pl.when((col == k) & down[0])(down[1].start)
            return carry

        lax.fori_loop(0, chunks, step, 0)

    def c_root(k):
        def step(c, carry):
            for cond, copy in c_sends(k, c):
                pl.when((row == k) & cond)(copy.start)
            return carry

        lax.fori_loop(0, chunks, step, 0)

    def r_wait(k, c):
        pl.when(keep(c))(remote(r_piece(k, c), r_send.at[k, 0, c], r_recv.at[k, c], (row, col)).wait_recv)

    def c_wait(k, c):
        remote(c_piece(k, c), c_send.at[k, 0, c], c_recv.at[k, c], (row, col)).wait_recv()

    def r_up(k, c):
        pl.when(keep(c))(r_sends(k, c)[0][1].start)

    middle = (col >= 1) & (col < n_col - 1)

    def r_early():
        def step(c, carry):
            r_wait(1, c)
            r_up(1, c)
            return carry

        lax.fori_loop(0, early, step, 0)

    def pump(s, tiles=True):
        if tiles:
            for i in (1, 2):
                pl.when((row != roots[i][0]) & (s == ring_hops[roots[i][0]]))(lambda i=i: d_relay(i))

        def r_one(c):
            r_wait(0, c)
            r_up(0, c)

            @pl.when(c < chunks - early)
            def _():
                pl.when(col > 1)(lambda: r_wait(1, c + early))
                r_up(1, c + early)

        u = s - col
        pl.when(middle & (u >= 0) & (u < 2 * chunks) & (lax.rem(u + 2 * n_col, 2) == 0))(lambda: r_one(u // 2))
        for k in range(2):
            def c_one(c, k=k):
                c_wait(k, c)
                for cond, copy in c_sends(k, c):
                    pl.when(cond)(copy.start)

            u = s - hops[k]
            pl.when((core == k) & (row != k) & (u >= 0) & (u < 2 * chunks) & (lax.rem(u + n_row, 2) == 0))(
                lambda c_one=c_one, u=u: c_one(u // 2))

    pl.when(row > 1)(lambda: [r_root(k) for k in range(2)] and None)
    pl.when((row > 1) & middle & (col > 1))(r_early)
    d_relay(0)
    pl.when(row == 1)(lambda: [d_relay(i) for i in (1, 2)] and None)
    pl.when(row <= 1)(lambda: [r_root(k) for k in range(2)] and None)
    for k in range(2):
        pl.when(row == k)(functools.partial(c_root, k))
    pl.when((row <= 1) & middle & (col > 1))(r_early)

    blocks = NB // BK
    set_work(work, dbuf[0])

    def first(s, carry):
        for q in range(STEPS):
            pump(s * STEPS + q)
        factor_block(work, lt_out.at[0], v_out.at[0], s)
        return carry

    lax.fori_loop(0, blocks, first, 0)
    most = half // 2 + 2
    if most > blocks * STEPS:
        def tiles_rest(s, carry):
            for i in (1, 2):
                pl.when((row != roots[i][0]) & (s == ring_hops[roots[i][0]]))(lambda i=i: d_relay(i))
            return carry

        lax.fori_loop(blocks * STEPS, most, tiles_rest, 0)
    mid = dot(dbuf[1], v_out[0], ((1,), (1,)))
    mid_out[...] = mid
    set_work(work, dbuf[2] - dot(mid, mid, ((1,), (1,))))

    def second(s, carry):
        for q in range(STEPS):
            pump((s + blocks) * STEPS + q, False)
        factor_block(work, lt_out.at[1], v_out.at[1], s)
        return carry

    lax.fori_loop(0, blocks, second, 0)

    total = 2 * chunks - 1 + max(n_col - 1, half)
    done = 2 * blocks * STEPS
    ahead = max(done, total - chunks) if chunks - 1 + half > done else done

    def rest(s, carry):
        pump(s, False)
        return carry

    if ahead > done:
        lax.fori_loop(done, ahead, rest, 0)

    def panels(c, carry):
        pump(ahead + c, False)
        for k in range(2):
            pl.when(core != k)(lambda k=k: c_wait(k, c))
        span = pl.ds(pl.multiple_of(c * c_step, c_step), c_step)
        p0 = halves(dot3(halves(v_out[0]), halves(cbuf[0, :, span])))
        left = cbuf[1, :, span] - dot3(halves(mid_out[...]), p0)
        p1 = halves(dot3(halves(v_out[1]), halves(left)))
        for k, (hi, lo) in enumerate((p0, p1)):
            right[pl.ds(3 * k * NB, NB), span] = hi
            right[pl.ds((3 * k + 1) * NB, NB), span] = lo
            right[pl.ds((3 * k + 2) * NB, NB), span] = hi
        return carry

    lax.fori_loop(0, chunks, panels, 0)
    if total > ahead + chunks:
        lax.fori_loop(ahead + chunks, total, rest, 0)
    c_back = local(right, c_out, loc.at[1])
    c_back.start()

    def ends(c, carry):
        pl.when(col == n_col - 1)(lambda: r_wait(0, c))
        pl.when((col == 0) | ((col == n_col - 1) & (col > 1)))(lambda: r_wait(1, c))
        return carry

    lax.fori_loop(0, chunks, ends, 0)

    back = [local(rbuf, r_out, loc.at[0])]
    for copy in back:
        copy.start()
    back.append(c_back)

    def d_drain(p, carry):
        for i in range(3):
            for cond, copy in d_sends(i, p)[1]:
                pl.when(cond)(copy.wait_send)
        return carry

    lax.fori_loop(0, PIECES, d_drain, 0)

    def drain(c, carry):
        for k in range(2):
            for cond, copy in r_sends(k, c) + c_sends(k, c):
                pl.when(cond)(copy.wait_send)
        return carry

    lax.fori_loop(0, chunks, drain, 0)
    for copy in back:
        copy.wait()


def halves(x):
    hi = x.astype(jnp.bfloat16)
    lo = (x - hi.astype(jnp.float32)).astype(jnp.bfloat16)
    return hi, lo


def dot3(a, b, dims=((1,), (0,))):
    part = lambda x, y: lax.dot_general(x, y, (dims, ((), ())), preferred_element_type=jnp.float32)
    return part(a[0], b[0]) + (part(a[0], b[1]) + part(a[1], b[0]))


def update_kernel(n_row, n_col, a_ref, r_ref, right, v_ref, lt_ref, mid_ref, o_ref):
    t = pl.program_id(0)
    row = lax.axis_index("row")
    col = lax.axis_index("col")
    n_cols = a_ref.shape[1]

    g = t * n_row + row
    across = ((1,), (1,))
    q0 = dot3(halves(r_ref[0]), halves(v_ref[0]), across)
    h0, l0 = halves(q0)
    rest = r_ref[1] - dot3((h0, l0), halves(mid_ref[...]), across)
    q1 = dot3(halves(rest), halves(v_ref[1]), across)
    h1, l1 = halves(q1)
    left = jnp.concatenate([h0, h0, l0, h1, h1, l1], axis=1)
    wide = 2 * NB if n_cols % (2 * NB) == 0 else NB

    @pl.loop(0, n_cols // wide)
    def _(s):
        span = pl.ds(pl.multiple_of(s * wide, wide), wide)
        o_ref[:, span] = a_ref[:, span] - lax.dot_general(
            left, right[:, span], (((1,), (0,)), ((), ())), preferred_element_type=jnp.float32)

    @pl.when(g < 2)
    def _():
        o_ref[...] = jnp.zeros_like(o_ref)

    @pl.when(col == 0)
    def _():
        o_ref[:, :NB] = q0

        @pl.when(g == 0)
        def _():
            o_ref[:, :NB] = lt_ref[0].T

    @pl.when((col == 1) & (g > 0))
    def _():
        o_ref[:, :NB] = q1

        @pl.when(g == 1)
        def _():
            o_ref[:, :NB] = lt_ref[1].T


def body(n_row, n_col, matrix):
    n_rows, n_cols = matrix.shape
    chunks = 10
    f32 = jnp.float32
    anyspace = pl.BlockSpec(memory_space=pl.ANY)
    vmem = pl.BlockSpec(memory_space=pltpu.VMEM)
    r, c, v, lt, mid = pl.pallas_call(
        functools.partial(chain_kernel, n_row, n_col, chunks),
        out_shape=(
            jax.ShapeDtypeStruct((2, n_rows, NB), f32),
            jax.ShapeDtypeStruct((6 * NB, n_cols), jnp.bfloat16),
            jax.ShapeDtypeStruct((2, NB, NB), f32),
            jax.ShapeDtypeStruct((2, NB, NB), f32),
            jax.ShapeDtypeStruct((NB, NB), f32),
        ),
        in_specs=[anyspace],
        out_specs=(anyspace, anyspace, vmem, vmem, vmem),
        scratch_shapes=[
            pltpu.VMEM((2, n_rows, NB), f32),
            pltpu.VMEM((2, NB, n_cols), f32),
            pltpu.VMEM((3, NB, NB), f32),
            pltpu.VMEM((NB, 2 * NB), f32),
            pltpu.SemaphoreType.DMA((2, 2, chunks)),
            pltpu.SemaphoreType.DMA((2, chunks)),
            pltpu.SemaphoreType.DMA((2, 2, chunks)),
            pltpu.SemaphoreType.DMA((2, chunks)),
            pltpu.SemaphoreType.DMA((3, 5, PIECES)),
            pltpu.SemaphoreType.DMA((3, PIECES)),
            pltpu.SemaphoreType.DMA((7,)),
            pltpu.VMEM((6 * NB, n_cols), jnp.bfloat16),
        ],
        compiler_params=pltpu.CompilerParams(
            collective_id=0, has_side_effects=True, vmem_limit_bytes=60 * 2**20),
        name="chain",
    )(matrix)
    whole = lambda shape: pl.BlockSpec(shape, lambda t: (0,) * len(shape), pipeline_mode=pl.Buffered(1))
    return pl.pallas_call(
        functools.partial(update_kernel, n_row, n_col),
        grid=(n_rows // NB,),
        out_shape=jax.ShapeDtypeStruct(matrix.shape, f32),
        in_specs=[
            pl.BlockSpec((NB, n_cols), lambda t: (t, 0)),
            pl.BlockSpec((2, NB, NB), lambda t: (0, t, 0)),
            whole((6 * NB, n_cols)),
            whole((2, NB, NB)),
            whole((2, NB, NB)),
            whole((NB, NB)),
        ],
        out_specs=pl.BlockSpec((NB, n_cols), lambda t: (t, 0)),
        compiler_params=pltpu.CompilerParams(vmem_limit_bytes=60 * 2**20),
        name="update",
    )(matrix, r, c, v, lt, mid)


def solution(mesh):
    n_row, n_col = mesh.shape["row"], mesh.shape["col"]
    return jax.shard_map(
        functools.partial(body, n_row, n_col), mesh=mesh,
        in_specs=(P("row", "col"),), out_specs=P("row", "col"), check_vma=False)
```
